128 devices in a mesh: comp: 16 (over x_lo, y, core), pair: 8 (over z, x_hi).
Axes of the slice: x: 4 (x_hi: 2, x_lo: 2; x = x_hi * 2 + x_lo), y: 4, z: 4, core: 2. Of those that a mesh axis runs over, the one named last changes fastest.
Arguments:
- densities: bfloat16 [8192, 65536], P('comp', 'pair'), may hold values from -6 to 6
- coulomb: float32 [8192], replicated, may hold values from 3.314563e-05 to 0.003314563
- pair_list: int32 [1024, 2], P(('comp', 'pair')), may hold values from 0 to 4095
- valence_energy: float32 [4096], replicated, may hold values from -20 to -0.5, as said below
- conduction_energy: float32 [4096], replicated, may hold values from 0.5 to 12, as said below
- tile_mask: int32 [512, 16], P(('pair', 'comp')), may hold values 0 or 1
Outputs:
- kernel: float32 [65536, 1024], P(('pair', 'comp'))
The draws below stay inside these ranges and needn't reach their ends.
Inputs may be any that keep to these rules, and one draw needn't show every extreme that they name: `valence_energy`: energies in electronvolts. `conduction_energy`: energies in electronvolts.
All inputs are finite; a program needn't handle non-finite values. No bound on the sum of `tile_mask` on one device may be relied on, other than what follows from the above.
Results may differ from the reference program's by a relative error of at most 0.0025.
Values may be sent and summed in bfloat16 or wider, within the bound.
No kernel may reach another device: no remote copies, remote signals or barrier semaphores. Data moves between devices by JAX's collectives and lax.ppermute only.
A program may use at most 128 MiB of HBM per device.

```python
import math
import jax
import jax.numpy as jnp
from jax import lax

NG = 8192
NWAN = 4096
TILE = 128
PAIR_DEV = 512
ROW_DEV = 8
NPAIR = 65536
ROWS = 1024
N_COMP = 16
N_PAIR = 8


def draw_valence_energy(key, part):
    level = jax.random.uniform(jax.random.fold_in(key, 11), (NWAN,), jnp.float32)
    return -0.5 - 19.5 * level


def draw_conduction_energy(key, part):
    level = jax.random.uniform(jax.random.fold_in(key, 23), (NWAN,), jnp.float32)
    return 0.5 + 11.5 * level


def place_ends(array, rng, low, largest):
    dims = array.shape
    spot = [jax.random.randint(jax.random.fold_in(rng, axis), (), 0, dims[axis]) for axis in range(len(dims))]
    array = array.at[tuple(spot)].set(low)
    longest = dims.index(max(dims))
    spot[longest] = (spot[longest] + 1) % dims[longest]
    return array.at[tuple(spot)].set(largest)


def block_scale(own_key, dims, cuts, smallest, largest):
    level = 1.0
    for axis_at, parts in cuts:
        steps = jax.random.uniform(jax.random.fold_in(jax.random.fold_in(own_key, 6), axis_at), (parts,), jnp.float32, smallest / len(cuts), largest / len(cuts))
        level = level * jnp.repeat(jnp.exp(steps), dims[axis_at] // parts).reshape((-1,) + (1,) * (len(dims) - 1 - axis_at))
    return level


def gaussian(stream_key, dims, scale, limit, split=(), kind=jnp.bfloat16):
    values = scale * jax.random.normal(stream_key, dims, jnp.float32)
    if split:
        values = values * block_scale(stream_key, dims, split, -0.22, 0.18)
    return jnp.clip(values, -limit, limit).astype(kind)


def setup_inputs(seed: int = 0) -> dict:
    seeds = jax.random.split(jax.random.key(seed), 7)
    densities = gaussian(seeds[0], (NG, NPAIR), 1.0, 6.0, ((0, 16), (1, 8)))
    coulomb = jnp.clip(jnp.exp(jax.random.uniform(seeds[1], (NG,), jnp.float32, math.log(3.3145628549391404e-05), math.log(0.003314563))), 3.3145628549391404e-05, 0.003314563)
    pair_list = place_ends(jax.random.randint(seeds[2], (ROWS, 2), 0, NWAN), jax.random.fold_in(seeds[2], 1), 0, NWAN - 1).astype(jnp.int32)
    valence_energy = draw_valence_energy(jax.random.fold_in(seeds[6], 71), 0)
    conduction_energy = draw_conduction_energy(jax.random.fold_in(seeds[6], 71), 0)
    tile_mask = place_ends((jax.random.randint(seeds[5], (NPAIR // TILE, N_COMP), 0, 4) < 3).astype(jnp.int32), jax.random.fold_in(seeds[5], 1), 0, 1)
    return dict(densities=densities, coulomb=coulomb, pair_list=pair_list, valence_energy=valence_energy, conduction_energy=conduction_energy, tile_mask=tile_mask)


def reference(densities, coulomb, pair_list, valence_energy, conduction_energy, tile_mask):
    blocks = densities.reshape(NG, N_PAIR, N_COMP, PAIR_DEV)[:, :, :, :ROW_DEV]
    rows = jnp.transpose(blocks, (2, 1, 3, 0)).reshape(ROWS, NG)
    panel = (rows.astype(jnp.float32) * coulomb[None, :]).astype(jnp.bfloat16)
    exchange = lax.dot_general(densities, panel, (((0,), (1,)), ((), ())), preferred_element_type=jnp.float32)
    masked = exchange.reshape(NPAIR // TILE, TILE, N_COMP, ROWS // N_COMP) * tile_mask.astype(jnp.float32)[:, None, :, None]
    masked = 2.0 * masked.reshape(NPAIR, ROWS)
    energy = conduction_energy[pair_list[:, 1]] - valence_energy[pair_list[:, 0]]
    index = jnp.arange(ROWS, dtype=jnp.int32)
    blk_c = index // (N_PAIR * ROW_DEV)
    blk_p = (index // ROW_DEV) % N_PAIR
    inner = index % ROW_DEV
    owner = (blk_p * N_COMP + blk_c) * PAIR_DEV + inner
    return masked.at[owner, index].add(energy)
```

```python
import functools

import jax
import jax.numpy as jnp
from jax import lax
from jax.experimental import pallas as pl
from jax.experimental.pallas import tpu as pltpu
from jax.sharding import PartitionSpec as P

TILE = 128
NX, NY, NC = 2, 4, 2
NZ, NH = 4, 2
N_COMP, N_PAIR = NX * NY * NC, NZ * NH
QB = 512
F32, BF16 = jnp.float32, jnp.bfloat16


def comp_at(x, y, k):
    return ((x % NX) * NY + y % NY) * NC + k % NC


def comp_perm(move):
    out = []
    for c in range(N_COMP):
        x, y, k = c // (NY * NC), (c // NC) % NY, c % NC
        out.append((c, comp_at(*move(x, y, k))))
    return out


CORE = comp_perm(lambda x, y, k: (x, y, k + 1))
XSWAP = comp_perm(lambda x, y, k: (x + 1, y, k))
XCROSS = comp_perm(lambda x, y, k: (x + 1, y, k + 1))
AHEAD = comp_perm(lambda x, y, k: (x, y + 1 - 2 * k, k))
BEHIND = comp_perm(lambda x, y, k: (x, y - 1 + 2 * k, k))
HALF = [(p, p ^ 1) for p in range(N_PAIR)]
ZSPLIT = [
    (c * N_PAIR + p, c * N_PAIR + ((p // NH + 1 - 2 * (c % NC)) % NZ) * NH + p % NH)
    for c in range(N_COMP)
    for p in range(N_PAIR)
]


def step_sign(b):
    return 1 - 2 * b[2]


def block_of(b, other_x, dy):
    x = 1 - b[0] if other_x else b[0]
    return (x * NY + ((b[1] + dy * step_sign(b) + NY) % NY)) * NC


def pick_kernel(b, *refs):
    blocks, (w_ref, o_ref) = refs[:-2], refs[-2:]
    sel = (
        lax.broadcasted_iota(jnp.int32, (8, 128), 0)
        == lax.broadcasted_iota(jnp.int32, (8, 128), 1)
    ).astype(BF16)
    for n, blk in enumerate(blocks):
        rows = lax.dot_general(
            sel, blk[...], (((1,), (1,)), ((), ())), preferred_element_type=F32
        )
        o_ref[8 * n : 8 * n + 8, :] = (rows * w_ref[0]).astype(BF16)


def pick(b, dens, coulomb):
    k = dens.shape[0]
    per = 4
    return pl.pallas_call(
        pick_kernel,
        grid_spec=pltpu.PrefetchScalarGridSpec(
            num_scalar_prefetch=1,
            grid=(N_COMP // per,),
            in_specs=[
                pl.BlockSpec((k, 128), lambda i, b, n=n: (0, (i * per + n) * (QB // 128)))
                for n in range(per)
            ]
            + [pl.BlockSpec((1, 1, k), lambda i, b: (b[3], 0, 0))],
            out_specs=pl.BlockSpec((8 * per, k), lambda i, b: (i, 0)),
        ),
        out_shape=jax.ShapeDtypeStruct((8 * N_COMP, k), BF16),
        name="pick",
    )(b, *([dens] * per), coulomb.reshape(N_COMP, 1, k))


def mm_kernel(parts, n_add, b, *refs):
    panels = refs[: 2 * parts]
    own, oth = refs[2 * parts : 2 * parts + 2]
    adds = refs[2 * parts + 2 : 2 * parts + 2 + n_add]
    o_ref = refs[-1]
    rows = panels[0].shape[0]
    for n in range(parts):
        acc = jnp.dot(panels[2 * n][...], own[...], preferred_element_type=F32)
        acc += jnp.dot(panels[2 * n + 1][...], oth[...], preferred_element_type=F32)
        at = slice(n * rows, (n + 1) * rows)
        for a in adds:
            acc += a[0, at, :].astype(F32)
        o_ref[0, at, :] = acc.astype(o_ref.dtype)


def mm(name, b, groups, dens, n, column, adds=(), dtype=BF16):
    own, oth = dens
    k = own.shape[0]
    rows = groups[0][0].shape[0]
    total = rows * len(groups)
    flat = [piece for pair in groups for piece in pair]
    return pl.pallas_call(
        functools.partial(mm_kernel, len(groups), len(adds)),
        grid_spec=pltpu.PrefetchScalarGridSpec(
            num_scalar_prefetch=1,
            grid=(n,),
            in_specs=[pl.BlockSpec((rows, k), lambda i, b: (0, 0)) for _ in flat]
            + [pl.BlockSpec((k, QB), lambda i, b: (0, column(i, b)))] * 2
            + [
                pl.BlockSpec((1, total, QB), lambda i, b, slot=slot: (slot(i, b), 0, 0))
                for _, slot in adds
            ],
            out_specs=pl.BlockSpec((1, total, QB), lambda i, b: (i, 0, 0)),
        ),
        out_shape=jax.ShapeDtypeStruct((n, total, QB), dtype),
        cost_estimate=pl.CostEstimate(
            flops=4 * n * total * k * QB,
            bytes_accessed=n * 4 * k * QB + n * total * QB * (2 + 2 * len(adds)),
            transcendentals=0,
        ),
        name=name,
    )(b, *flat, own, oth, *[a for a, _ in adds])


def final_kernel(b, mask, xo, xr, yo, yr, fo, fr, diag, o_ref, t_ref):
    z, half, core = b[4], b[5], b[2]

    def pair_at(dz, dh):
        return ((z + dz + NZ) % NZ) * NH + (half + dh) % NH

    def place(value, row, c, p):
        for t in range(QB // TILE):
            scale = (2 * mask[t, c]).astype(F32)
            at = pl.ds(pl.multiple_of((c * N_PAIR + p) * 8, 8), 8)
            t_ref[at, t * TILE : (t + 1) * TILE] = value(t) * scale

    order = (((0, 0), (-1, 0), (-1, 1), (-2, 0)), ((0, 1), (1, 1), (1, 0), (2, 1)))
    for source in range(2):
        mine = source == 0
        for g in range(4):
            spots = [pair_at(*order[s][g]) for s in range(2)]
            same = core if mine else 1 - core
            p = jnp.where(same == 0, spots[0], spots[1])
            for c in range(N_COMP):
                row = (g % 2) * 128 + c * 8
                if g < 2:
                    src = xo if mine else xr
                    value = lambda t, src=src, row=row: src[
                        0, row : row + 8, t * TILE : (t + 1) * TILE
                    ]
                else:
                    src, more = (yo, fo) if mine else (yr, fr)
                    value = lambda t, src=src, more=more, row=row: src[
                        0, row : row + 8, t * TILE : (t + 1) * TILE
                    ] + more[0, row : row + 8, t * TILE : (t + 1) * TILE].astype(F32)
                place(value, row, c, p)
    here = pl.ds(pl.multiple_of((b[3] * N_PAIR + pair_at(0, 0)) * 8, 8), 8)
    t_ref[here, 0:TILE] = t_ref[here, 0:TILE] + diag[...]
    o_ref[...] = t_ref[...].T


def final(b, mask, parts, diag):
    window = 8 * N_COMP * N_PAIR
    full = lambda a: pl.BlockSpec(a.shape, lambda i, b, m: (0,) * a.ndim)
    return pl.pallas_call(
        final_kernel,
        grid_spec=pltpu.PrefetchScalarGridSpec(
            num_scalar_prefetch=2,
            grid=(1,),
            in_specs=[full(a) for a in parts] + [full(diag)],
            out_specs=pl.BlockSpec((QB, window), lambda i, b, m: (0, 0)),
            scratch_shapes=[pltpu.VMEM((window, QB), F32)],
        ),
        out_shape=jax.ShapeDtypeStruct((QB, window), F32),
        name="final",
    )(b, mask, *parts, diag)


def energy_tile(pair_list, valence_energy, conduction_energy):
    table = jnp.arange(valence_energy.shape[0], dtype=jnp.int32)
    cond_hits = pair_list[:, 1][:, None] == table[None, :]
    val_hits = pair_list[:, 0][:, None] == table[None, :]
    energy = jnp.sum(jnp.where(cond_hits, conduction_energy[None, :], 0.0), axis=1) - jnp.sum(
        jnp.where(val_hits, valence_energy[None, :], 0.0), axis=1
    )
    return jnp.eye(8, TILE, dtype=F32) * energy[:, None]


def per_device(densities, coulomb, pair_list, valence_energy, conduction_energy, tile_mask):
    comp = lax.axis_index("comp")
    pair = lax.axis_index("pair")
    core = comp % NC
    pos = jnp.arange(8, dtype=jnp.int32)
    facts = (comp // (NY * NC), (comp // NC) % NY, core, comp, pair // NH, pair % NH)
    b = jnp.zeros((8,), jnp.int32)
    for n, fact in enumerate(facts):
        b = jnp.where(pos == n, fact, b)

    swap = lambda a: lax.ppermute(a, "comp", CORE)
    dens = (densities, swap(densities))

    with jax.named_scope("panel"):
        v = pick(b, densities, coulomb)
        hv = lax.ppermute(v, "pair", HALF)
        mine = jnp.stack([v, hv])
        theirs = swap(mine)
        mine = jnp.where(core == 0, mine, mine[::-1])
        theirs = jnp.where(core == 0, theirs, theirs[::-1])
        first = jnp.stack([mine[0], theirs[0]])
        second = jnp.stack([mine[1], theirs[1]])
        zmove = lambda a: lax.ppermute(a, ("comp", "pair"), ZSPLIT)
        near = zmove(first)
        near2 = zmove(second)
        far = zmove(near)
    rows_x = [(first[0], first[1]), (near[0], near[1])]
    rows_y = [(near2[0], near2[1]), (far[0], far[1])]

    def dests(*pairs):
        def column(i, b):
            out = block_of(b, *pairs[-1])
            for n in range(len(pairs) - 2, -1, -1):
                out = jnp.where(i // NC == n, block_of(b, *pairs[n]), out)
            return out + i % NC

        return column

    same = lambda i, b: i
    ahead = lambda a: lax.ppermute(a, "comp", AHEAD)
    behind = lambda a: lax.ppermute(a, "comp", BEHIND)

    with jax.named_scope("x_then_y_send"):
        x1 = mm("x1", b, rows_x, dens, 4, dests((True, 2), (True, -1)))
        x1r = lax.ppermute(x1, "comp", XSWAP)
        x2 = mm("x2", b, rows_x, dens, 4, dests((True, 1), (True, 0)))
        x2r = lax.ppermute(x2, "comp", XSWAP)
    with jax.named_scope("y_then_x"):
        m1y = ahead(mm("m1y", b, rows_y, dens, 4, dests((True, 2), (False, 2))))
        m2y = behind(mm("m2y", b, rows_y, dens, 4, dests((True, -1), (False, -1))))
        m3y = ahead(
            mm("m3y", b, rows_y, dens, 4, dests((True, 1), (False, 1)), [(m1y, same)])
        )
    with jax.named_scope("x_then_y"):
        m1x = ahead(mm("m1x", b, rows_x, dens, 2, dests((False, 2)), [(x1r, same)]))
        m2x = behind(
            mm("m2x", b, rows_x, dens, 2, dests((False, -1)), [(x1r, lambda i, b: i + 2)])
        )
        m3x = ahead(
            mm("m3x", b, rows_x, dens, 2, dests((False, 1)), [(x2r, same), (m1x, same)])
        )

    mine_at = lambda i, b: b[2]
    other_at = lambda i, b: 1 - b[2]

    def at(core_of, base):
        return lambda i, b: base + core_of(i, b)

    def last_x(name, core_of):
        return mm(
            name, b, rows_x, dens, 1,
            lambda i, b: block_of(b, False, 0) + core_of(i, b),
            [(x2r, at(core_of, 2)), (m3x, at(core_of, 0)), (m2x, at(core_of, 0))],
            F32,
        )

    def last_y(name, core_of, other_x, dtype):
        base = 0 if other_x else 2
        return mm(
            name, b, rows_y, dens, 1,
            lambda i, b: block_of(b, other_x, 0) + core_of(i, b),
            [(m3y, at(core_of, base)), (m2y, at(core_of, base))],
            dtype,
        )

    with jax.named_scope("last"):
        fo = lax.ppermute(last_y("yf", mine_at, True, BF16), "comp", XSWAP)
        fr = lax.ppermute(last_y("yg", other_at, True, BF16), "comp", XCROSS)
        yr = swap(last_y("ys", other_at, False, F32))
        yo = last_y("yo", mine_at, False, F32)
        xr = swap(last_x("xs", other_at))
        xo = last_x("xo", mine_at)
        diag = energy_tile(pair_list, valence_energy, conduction_energy)
        return final(b, tile_mask, (xo, xr, yo, yr, fo, fr), diag)


def solution(mesh):
    return jax.shard_map(
        per_device,
        mesh=mesh,
        in_specs=(
            P("comp", "pair"),
            P(),
            P(("comp", "pair"), None),
            P(),
            P(),
            P(("pair", "comp"), None),
        ),
        out_specs=P(("pair", "comp"), None),
        check_vma=False,
    )
```

```python
import functools

import jax
import jax.numpy as jnp
from jax import lax
from jax.experimental import pallas as pl
from jax.experimental.pallas import tpu as pltpu
from jax.sharding import PartitionSpec as P

TILE = 128
NX, NY, NC = 2, 4, 2
NZ, NH = 4, 2
N_COMP, N_PAIR = NX * NY * NC, NZ * NH
QB = 512
F32, BF16 = jnp.float32, jnp.bfloat16


def comp_at(x, y, k):
    return ((x % NX) * NY + y % NY) * NC + k % NC


def comp_perm(move):
    out = []
    for c in range(N_COMP):
        x, y, k = c // (NY * NC), (c // NC) % NY, c % NC
        out.append((c, comp_at(*move(x, y, k))))
    return out


CORE = comp_perm(lambda x, y, k: (x, y, k + 1))
XSWAP = comp_perm(lambda x, y, k: (x + 1, y, k))
XCROSS = comp_perm(lambda x, y, k: (x + 1, y, k + 1))
AHEAD = comp_perm(lambda x, y, k: (x, y + 1 - 2 * k, k))
BEHIND = comp_perm(lambda x, y, k: (x, y - 1 + 2 * k, k))
HALF = [(p, p ^ 1) for p in range(N_PAIR)]
ZSPLIT = [
    (c * N_PAIR + p, c * N_PAIR + ((p // NH + 1 - 2 * (c % NC)) % NZ) * NH + p % NH)
    for c in range(N_COMP)
    for p in range(N_PAIR)
]


def place_facts():
    comp, pair = lax.axis_index("comp"), lax.axis_index("pair")
    return [comp // (NY * NC), (comp // NC) % NY, comp % NC, comp, pair // NH, pair % NH]


def step_sign(b):
    return 1 - 2 * b[2]


def block_of(b, other_x, dy):
    x = 1 - b[0] if other_x else b[0]
    return (x * NY + ((b[1] + dy * step_sign(b) + NY) % NY)) * NC


VMEM = pl.BlockSpec(memory_space=pltpu.VMEM)
ANY = pl.BlockSpec(memory_space=pl.ANY)
HBM = pl.BlockSpec(memory_space=pltpu.HBM)
LIMIT = 20 << 20
NO_ROOM = 58 << 20


def pick_kernel(dens, w_ref, o_ref, buf, sems):
    def load(n):
        return pltpu.make_async_copy(
            dens.at[:, n * QB : n * QB + TILE], buf.at[:, n * TILE : (n + 1) * TILE], sems.at[n]
        )

    for n in range(N_COMP):
        load(n).start()
    k, wide = buf.shape
    at = lax.broadcasted_iota(jnp.int32, (wide, TILE), 0)
    to = lax.broadcasted_iota(jnp.int32, (wide, TILE), 1)
    spots = (at == (to // 8) * TILE + to % 8).astype(BF16)
    per = k // TILE
    comp = lax.axis_index("comp")
    w = [w_ref[pl.ds(comp * per + n, 1), :] for n in range(per)]
    for n in range(N_COMP):
        load(n).wait()
    rows = jnp.dot(buf[...], spots, preferred_element_type=F32)
    o_ref[0] = (rows.T * jnp.concatenate(w, axis=1)).astype(BF16)


def pick(dens, coulomb):
    k = dens.shape[0]
    return pl.pallas_call(
        pick_kernel,
        in_specs=[HBM, VMEM],
        out_specs=VMEM,
        out_shape=jax.ShapeDtypeStruct((1, 8 * N_COMP, k), BF16),
        scratch_shapes=[
            pltpu.VMEM((k, N_COMP * TILE), BF16),
            pltpu.SemaphoreType.DMA((N_COMP,)),
        ],
        compiler_params=pltpu.CompilerParams(vmem_limit_bytes=NO_ROOM),
        name="pick",
    )(dens, coulomb.reshape(coulomb.shape[0] // TILE, TILE))


def pair_kernel(a_ref, b_ref, o_ref, same_ref):
    for out in (o_ref, same_ref):
        out[0:1] = a_ref[...]
        out[1:2] = b_ref[...]


def pair_up(a, b):
    return pl.pallas_call(
        pair_kernel,
        in_specs=[VMEM, VMEM],
        out_specs=[VMEM, VMEM],
        out_shape=[jax.ShapeDtypeStruct((2, *a.shape[1:]), a.dtype)] * 2,
        compiler_params=pltpu.CompilerParams(vmem_limit_bytes=LIMIT),
        name="pair_up",
    )(a, b)


def choose_kernel(zero, one, after, o_ref):
    o_ref[...] = jnp.where(place_facts()[2] == 0, zero[...], one[...])


def choose(zero, one, after):
    return pl.pallas_call(
        choose_kernel,
        in_specs=[VMEM, VMEM, ANY],
        out_specs=VMEM,
        out_shape=jax.ShapeDtypeStruct(zero.shape, zero.dtype),
        compiler_params=pltpu.CompilerParams(vmem_limit_bytes=LIMIT),
        name="choose",
    )(zero, one, after)


def mm_kernel(work, sizes, n_add, n_out, *refs):
    n_panel = sum(sizes)
    panels, (own, oth), refs = refs[:n_panel], refs[n_panel : n_panel + 2], refs[n_panel + 2 :]
    adds, outs = refs[:n_add], refs[n_add : n_add + n_out]
    own_buf, oth_buf, sems = refs[-3:]
    b = place_facts()

    def loads(n):
        at = pl.ds(pl.multiple_of(work[n][2](b) * QB, QB), QB)
        return [
            pltpu.make_async_copy(src.at[:, at], buf.at[n], sems.at[s, n])
            for s, (src, buf) in enumerate(((own, own_buf), (oth, oth_buf)))
        ]

    for n in range(len(work)):
        for copy in loads(n):
            copy.start()
    sides = ([], [])
    for size in sizes:
        group, panels = panels[:size], panels[size:]
        for n, side in enumerate(sides):
            if size == 1:
                side.append(group[0][n])
            else:
                side.append(jnp.where(b[2] == 0, group[0][n], group[1][n]))
    left, right = [jnp.concatenate(side) if len(side) > 1 else side[0] for side in sides]
    rows = left.shape[0]
    part = rows // len(sizes)
    for n, (out, slot, _, terms) in enumerate(work):
        for copy in loads(n):
            copy.wait()
        acc = jnp.dot(left, own_buf[n], preferred_element_type=F32)
        acc += jnp.dot(right, oth_buf[n], preferred_element_type=F32)
        for g in range(len(sizes)):
            piece = acc[g * part : (g + 1) * part]
            for a, where in terms:
                if isinstance(a, tuple):
                    piece += adds[a[g]][where(b)].astype(F32)
                else:
                    piece += adds[a][where(b), g * part : (g + 1) * part].astype(F32)
            if isinstance(out, tuple):
                step = rows // len(out)
                for m in range(g * part // step, (g + 1) * part // step):
                    outs[out[m]][slot] = piece[m * step - g * part : (m + 1) * step - g * part]
            else:
                outs[out][slot, g * part : (g + 1) * part] = piece.astype(outs[out].dtype)


def mm(name, groups, dens, work, outs, adds=(), after=(), limit=LIMIT):
    k = dens[0].shape[0]
    rows = 128 * len(groups)
    n = len(work)
    panels = [piece for group in groups for piece in group]

    def body(*refs):
        n_in = len(panels) + 2 + len(adds)
        mm_kernel(
            work, [len(g) for g in groups], len(adds), len(outs), *refs[:n_in], *refs[n_in + len(after) :]
        )

    return pl.pallas_call(
        body,
        in_specs=[VMEM] * len(panels) + [HBM] * 2 + [VMEM] * len(adds) + [ANY] * len(after),
        out_specs=[VMEM] * len(outs),
        out_shape=[jax.ShapeDtypeStruct((m, out_rows or rows, QB), dtype) for m, dtype, out_rows in outs],
        scratch_shapes=[pltpu.VMEM((n, k, QB), BF16)] * 2 + [pltpu.SemaphoreType.DMA((2, n))],
        cost_estimate=pl.CostEstimate(
            flops=4 * n * rows * k * QB, bytes_accessed=4 * n * k * QB, transcendentals=0
        ),
        compiler_params=pltpu.CompilerParams(vmem_limit_bytes=limit),
        name=name,
    )(*panels, *dens, *adds, *after)


def final_kernel(mask, *refs):
    b = place_facts()
    z, half, core = b[4], b[5], b[2]
    (xo, *xr), (yo, *yr), (fo, fr, diag, o_ref, t_ref) = refs[:5], refs[5:10], refs[10:]

    def pair_at(dz, dh):
        return ((z + dz + NZ) % NZ) * NH + (half + dh) % NH

    def place(value, c, p):
        for t in range(QB // TILE):
            scale = (2 * mask[t, c]).astype(F32)
            at = pl.ds(pl.multiple_of((c * N_PAIR + p) * 8, 8), 8)
            t_ref[at, t * TILE : (t + 1) * TILE] = value(t) * scale

    order = (((-1, 1), (-2, 0), (0, 0), (-1, 0)), ((1, 1), (2, 1), (0, 1), (1, 0)))
    for source in range(2):
        mine = source == 0
        for g in range(4):
            spots = [pair_at(*order[s][g]) for s in range(2)]
            same = core if mine else 1 - core
            p = jnp.where(same == 0, spots[0], spots[1])
            for c in range(N_COMP):
                row = (g % 2) * 128 + c * 8
                own, swapped, more = (xo, xr, None) if g < 2 else (yo, yr, fo if mine else fr)
                if mine:
                    src, at = own, row
                else:
                    src, at = swapped[row // 64], row % 64

                def value(t, src=src, at=at, more=more, row=row):
                    lanes = slice(t * TILE, (t + 1) * TILE)
                    out = src[0, at : at + 8, lanes]
                    if more is not None:
                        out = out + more[0, row : row + 8, lanes].astype(F32)
                    return out

                place(value, c, p)
    here = pl.ds(pl.multiple_of((b[3] * N_PAIR + pair_at(0, 0)) * 8, 8), 8)
    t_ref[here, 0:TILE] = t_ref[here, 0:TILE] + diag[...]
    o_ref[...] = t_ref[...].T


def final(mask, parts, diag):
    window = 8 * N_COMP * N_PAIR
    return pl.pallas_call(
        final_kernel,
        in_specs=[pl.BlockSpec(memory_space=pltpu.SMEM)] + [VMEM] * (len(parts) + 1),
        out_specs=VMEM,
        out_shape=jax.ShapeDtypeStruct((QB, window), F32),
        scratch_shapes=[pltpu.VMEM((window, QB), F32)],
        compiler_params=pltpu.CompilerParams(vmem_limit_bytes=LIMIT),
        name="final",
    )(mask, *parts, diag)


def energy_tile(pair_list, valence_energy, conduction_energy):
    table = jnp.arange(valence_energy.shape[0], dtype=jnp.int32)
    cond_hits = pair_list[:, 1][:, None] == table[None, :]
    val_hits = pair_list[:, 0][:, None] == table[None, :]
    energy = jnp.sum(jnp.where(cond_hits, conduction_energy[None, :], 0.0), axis=1) - jnp.sum(
        jnp.where(val_hits, valence_energy[None, :], 0.0), axis=1
    )
    return jnp.eye(8, TILE, dtype=F32) * energy[:, None]


def per_device(densities, coulomb, pair_list, valence_energy, conduction_energy, tile_mask):
    swap = lambda a: lax.ppermute(a, "comp", CORE)
    zmove = lambda a: lax.ppermute(a, ("comp", "pair"), ZSPLIT)
    with jax.named_scope("panel"):
        v = pick(densities, coulomb)
        w = swap(v)
        held, w = lax.optimization_barrier((densities, w))
        dens = (densities, swap(held))
        vw, vw_again = pair_up(v, w)
        hvw = lax.ppermute(vw_again, "pair", HALF)
        near = zmove(vw)
        near2 = zmove(hvw)
    early = (vw, hvw)

    ahead = lambda a: lax.ppermute(a, "comp", AHEAD)
    behind = lambda a: lax.ppermute(a, "comp", BEHIND)
    across = lambda a: lax.ppermute(a, "comp", XSWAP)

    def both(out, start, other_x, dy, terms=()):
        return [
            (
                out, start + n,
                lambda b, n=n: block_of(b, other_x, dy) + n,
                tuple((a, lambda b, t=t, n=n: t + n) for a, t in terms),
            )
            for n in range(NC)
        ]

    def each(out_mine, out_other, other_x, terms):
        mine, other = lambda b: b[2], lambda b: 1 - b[2]
        return [
            (
                out, 0,
                lambda b, core=core: block_of(b, other_x, 0) + core(b),
                tuple((a, lambda b, t=t, core=core: t + core(b)) for a, t in terms),
            )
            for out, core in ((out_mine, mine), (out_other, other))
        ]

    def mmx(name, *rest, **more):
        return mm(name, [(near2,), (far,)], dens, *rest, **more)

    def mmy(name, *rest, **more):
        return mm(name, [early, (near,)], dens, *rest, **more)

    def through_y(other_x, **more):
        dest = lambda out, start, dy: both(out, start, other_x, dy)
        m1, m2 = mmy("m12y", dest(0, 0, 2) + dest(1, 0, -1), [(2, BF16, 0)] * 2, **more)
        return m1, ahead(m1), behind(m2)

    def through_y_2(other_x, m1r, after):
        m3, = mmy("m3y", both(0, 0, other_x, 1, [(0, 0)]), [(2, BF16, 0)], [m1r], after=after)
        return m3, ahead(m3)

    near_dests = both(0, 0, True, 2) + both(0, 2, True, -1)
    with jax.named_scope("y_then_x"):
        m1o, m1or, m2or = through_y(True)
    with jax.named_scope("x_then_y_send"):
        far = zmove(choose(near, near2, m1o))
        xe, = mm("xe", [(near2,)], dens, near_dests, [(4, BF16, 0)], after=(m1o,))
        xer = across(xe)
    with jax.named_scope("y_then_x"):
        m1w, m1wr, m2wr = through_y(False, after=(xe,))
    with jax.named_scope("x_then_y_send"):
        xl, = mm("xl", [(far,)], dens, near_dests, [(4, BF16, 0)], after=(m1w,))
        xlr = across(xl)
        x2, = mmx("x2", both(0, 0, True, 1) + both(0, 2, True, 0), [(4, BF16, 0)], after=(xl,))
        x2r = across(x2)
    with jax.named_scope("y_then_x"):
        m3o, m3or = through_y_2(True, m1or, (x2, xer))
        m3w, m3wr = through_y_2(False, m1wr, (m3o,))
        yf, yg = mmy(
            "yfg", each(0, 1, True, [(0, 0), (1, 0)]), [(1, BF16, 0)] * 2, [m3or, m2or], after=(m3w, xlr)
        )
        fo, fr = across(yf), lax.ppermute(yg, "comp", XCROSS)
    with jax.named_scope("x_then_y"):
        m1x, m2x = mmx(
            "m12x", both(0, 0, False, 2, [((0, 1), 0)]) + both(1, 0, False, -1, [((0, 1), 2)]),
            [(2, BF16, 0)] * 2, [xer, xlr], after=(yf,),
        )
        m1xr, m2xr = ahead(m1x), behind(m2x)
        m3x, = mmx(
            "m3x", both(0, 0, False, 1, [(0, 0), (1, 0)]), [(2, BF16, 0)], [x2r, m1xr], after=(m1x,)
        )
        m3xr = ahead(m3x)

    split = [(1, F32, 0)] + [(1, F32, 64)] * 4
    with jax.named_scope("last"):
        yo, *ys = mmy(
            "yos", each(0, (1, 2, 3, 4), False, [(0, 0), (1, 0)]), split, [m3wr, m2wr], after=(m3x,)
        )
        yr = [swap(a) for a in ys]
        xo, *xs = mmx(
            "xos", each(0, (1, 2, 3, 4), False, [(0, 2), (1, 0), (2, 0)]), split, [x2r, m3xr, m2xr],
            after=(yo,),
        )
        xr = [swap(a) for a in xs]
        diag = energy_tile(pair_list, valence_energy, conduction_energy)
        return final(tile_mask, (xo, *xr, yo, *yr, fo, fr), diag)


def solution(mesh):
    return jax.shard_map(
        per_device,
        mesh=mesh,
        in_specs=(
            P("comp", "pair"),
            P(),
            P(("comp", "pair"), None),
            P(),
            P(),
            P(("pair", "comp"), None),
        ),
        out_specs=P(("pair", "comp"), None),
        check_vma=False,
    )
```

```python
import functools

import jax
import jax.numpy as jnp
from jax import lax
from jax.experimental import pallas as pl
from jax.experimental.pallas import tpu as pltpu
from jax.sharding import PartitionSpec as P

TILE = 128
NX, NY, NC = 2, 4, 2
NZ, NH = 4, 2
N_COMP, N_PAIR = NX * NY * NC, NZ * NH
QB = 512
F32, BF16 = jnp.float32, jnp.bfloat16


def comp_at(x, y, k):
    return ((x % NX) * NY + y % NY) * NC + k % NC


def comp_perm(move):
    out = []
    for c in range(N_COMP):
        x, y, k = c // (NY * NC), (c // NC) % NY, c % NC
        out.append((c, comp_at(*move(x, y, k))))
    return out


CORE = comp_perm(lambda x, y, k: (x, y, k + 1))
XSWAP = comp_perm(lambda x, y, k: (x + 1, y, k))
XCROSS = comp_perm(lambda x, y, k: (x + 1, y, k + 1))
AHEAD = comp_perm(lambda x, y, k: (x, y + 1 - 2 * k, k))
BEHIND = comp_perm(lambda x, y, k: (x, y - 1 + 2 * k, k))
HALF = [(p, p ^ 1) for p in range(N_PAIR)]
ZSPLIT = [
    (c * N_PAIR + p, c * N_PAIR + ((p // NH + 1 - 2 * (c % NC)) % NZ) * NH + p % NH)
    for c in range(N_COMP)
    for p in range(N_PAIR)
]


def place_facts():
    comp, pair = lax.axis_index("comp"), lax.axis_index("pair")
    return [comp // (NY * NC), (comp // NC) % NY, comp % NC, comp, pair // NH, pair % NH]


def step_sign(b):
    return 1 - 2 * b[2]


def block_of(b, other_x, dy):
    x = 1 - b[0] if other_x else b[0]
    return (x * NY + ((b[1] + dy * step_sign(b) + NY) % NY)) * NC


VMEM = pl.BlockSpec(memory_space=pltpu.VMEM)
ANY = pl.BlockSpec(memory_space=pl.ANY)
HBM = pl.BlockSpec(memory_space=pltpu.HBM)
LIMIT = 20 << 20
NO_ROOM = 58 << 20


def pick_kernel(dens, w_ref, o_ref, buf, sems):
    def load(n):
        return pltpu.make_async_copy(
            dens.at[:, n * QB : n * QB + TILE], buf.at[:, n * TILE : (n + 1) * TILE], sems.at[n]
        )

    for n in range(N_COMP):
        load(n).start()
    k, wide = buf.shape
    at = lax.broadcasted_iota(jnp.int32, (wide, TILE), 0)
    to = lax.broadcasted_iota(jnp.int32, (wide, TILE), 1)
    spots = (at == (to // 8) * TILE + to % 8).astype(BF16)
    per = k // TILE
    comp = lax.axis_index("comp")
    w = [w_ref[pl.ds(comp * per + n, 1), :] for n in range(per)]
    for n in range(N_COMP):
        load(n).wait()
    rows = jnp.dot(buf[...], spots, preferred_element_type=F32)
    o_ref[0] = (rows.T * jnp.concatenate(w, axis=1)).astype(BF16)


def pick(dens, coulomb):
    k = dens.shape[0]
    return pl.pallas_call(
        pick_kernel,
        in_specs=[HBM, VMEM],
        out_specs=VMEM,
        out_shape=jax.ShapeDtypeStruct((1, 8 * N_COMP, k), BF16),
        scratch_shapes=[
            pltpu.VMEM((k, N_COMP * TILE), BF16),
            pltpu.SemaphoreType.DMA((N_COMP,)),
        ],
        compiler_params=pltpu.CompilerParams(vmem_limit_bytes=LIMIT),
        name="pick",
    )(dens, coulomb.reshape(coulomb.shape[0] // TILE, TILE))


def pair_kernel(a_ref, b_ref, o_ref, same_ref):
    for out in (o_ref, same_ref):
        out[0:1] = a_ref[...]
        out[1:2] = b_ref[...]


def pair_up(a, b):
    return pl.pallas_call(
        pair_kernel,
        in_specs=[VMEM, VMEM],
        out_specs=[VMEM, VMEM],
        out_shape=[jax.ShapeDtypeStruct((2, *a.shape[1:]), a.dtype)] * 2,
        compiler_params=pltpu.CompilerParams(vmem_limit_bytes=LIMIT),
        name="pair_up",
    )(a, b)


def choose_kernel(zero, one, after, o_ref):
    o_ref[...] = jnp.where(place_facts()[2] == 0, zero[...], one[...])


def choose(zero, one, after):
    return pl.pallas_call(
        choose_kernel,
        in_specs=[VMEM, VMEM, ANY],
        out_specs=VMEM,
        out_shape=jax.ShapeDtypeStruct(zero.shape, zero.dtype),
        compiler_params=pltpu.CompilerParams(vmem_limit_bytes=LIMIT),
        name="choose",
    )(zero, one, after)


def mm_kernel(work, sizes, n_add, n_out, *refs):
    n_panel = sum(sizes)
    panels, (own, oth), refs = refs[:n_panel], refs[n_panel : n_panel + 2], refs[n_panel + 2 :]
    adds, outs = refs[:n_add], refs[n_add : n_add + n_out]
    own_buf, oth_buf, sems = refs[-3:]
    b = place_facts()

    def loads(n):
        at = pl.ds(pl.multiple_of(work[n][2](b) * QB, QB), QB)
        return [
            pltpu.make_async_copy(src.at[:, at], buf.at[n], sems.at[s, n])
            for s, (src, buf) in enumerate(((own, own_buf), (oth, oth_buf)))
        ]

    for n in range(len(work)):
        for copy in loads(n):
            copy.start()
    sides = ([], [])
    for size in sizes:
        group, panels = panels[:size], panels[size:]
        for n, side in enumerate(sides):
            if size == 1:
                side.append(group[0][n])
            else:
                side.append(jnp.where(b[2] == 0, group[0][n], group[1][n]))
    left, right = [jnp.concatenate(side) if len(side) > 1 else side[0] for side in sides]
    rows = left.shape[0]
    part = rows // len(sizes)
    for n, (out, slot, _, terms) in enumerate(work):
        for copy in loads(n):
            copy.wait()
        acc = jnp.dot(left, own_buf[n], preferred_element_type=F32)
        acc += jnp.dot(right, oth_buf[n], preferred_element_type=F32)
        for g in range(len(sizes)):
            piece = acc[g * part : (g + 1) * part]
            for a, where in terms:
                if isinstance(a, tuple):
                    piece += adds[a[g]][where(b, g)].astype(F32)
                else:
                    piece += adds[a][where(b), g * part : (g + 1) * part].astype(F32)
            if isinstance(out, tuple):
                step = rows // len(out)
                for m in range(g * part // step, (g + 1) * part // step):
                    outs[out[m]][slot] = piece[m * step - g * part : (m + 1) * step - g * part]
            elif isinstance(slot, tuple):
                if slot[g] is not None:
                    outs[out][slot[g]] = piece.astype(outs[out].dtype)
            else:
                outs[out][slot, g * part : (g + 1) * part] = piece.astype(outs[out].dtype)


def mm(name, groups, dens, work, outs, adds=(), after=(), limit=LIMIT, weight=1):
    k = dens[0].shape[0]
    rows = 128 * len(groups)
    n = len(work)
    panels = [piece for group in groups for piece in group]

    def body(*refs):
        n_in = len(panels) + 2 + len(adds)
        mm_kernel(
            work, [len(g) for g in groups], len(adds), len(outs), *refs[:n_in], *refs[n_in + len(after) :]
        )

    return pl.pallas_call(
        body,
        in_specs=[VMEM] * len(panels) + [HBM] * 2 + [VMEM] * len(adds) + [ANY] * len(after),
        out_specs=[VMEM] * len(outs),
        out_shape=[jax.ShapeDtypeStruct((m, out_rows or rows, QB), dtype) for m, dtype, out_rows in outs],
        scratch_shapes=[pltpu.VMEM((n, k, QB), BF16)] * 2 + [pltpu.SemaphoreType.DMA((2, n))],
        cost_estimate=pl.CostEstimate(
            flops=4 * n * rows * k * QB * weight, bytes_accessed=4 * n * k * QB, transcendentals=0
        ),
        compiler_params=pltpu.CompilerParams(vmem_limit_bytes=limit),
        name=name,
    )(*panels, *dens, *adds, *after)


ORDER = (((-1, 1), (-2, 0), (0, 0), (-1, 0)), ((1, 1), (2, 1), (0, 1), (1, 0)))


def place_rows(b, mask, t_ref, groups, sources):
    for source, rows_at in enumerate(sources):
        for n, g in enumerate(groups):
            spots = [
                ((b[4] + ORDER[s][g][0] + NZ) % NZ) * NH + (b[5] + ORDER[s][g][1]) % NH
                for s in range(2)
            ]
            same = b[2] if source == 0 else 1 - b[2]
            p = jnp.where(same == 0, spots[0], spots[1])
            for c in range(N_COMP):
                at = pl.ds(pl.multiple_of((c * N_PAIR + p) * 8, 8), 8)
                for t in range(QB // TILE):
                    lanes = slice(t * TILE, (t + 1) * TILE)
                    scale = (2 * mask[t, c]).astype(F32)
                    t_ref[at, lanes] = rows_at(n, c * 8, lanes) * scale


def gather_y_kernel(mask, yo, ya, yb, fo, fr, t_ref):
    def mine(n, at, lanes):
        row = slice(n * 128 + at, n * 128 + at + 8)
        return yo[0, row, lanes] + fo[0, row, lanes].astype(F32)

    def others(n, at, lanes):
        row = slice(n * 128 + at, n * 128 + at + 8)
        return (ya, yb)[n][0, at : at + 8, lanes] + fr[0, row, lanes].astype(F32)

    place_rows(place_facts(), mask, t_ref, (2, 3), (mine, others))


def final_kernel(mask, y_rows, xo, xa, xb, diag, o_ref, t_ref):
    b = place_facts()
    t_ref[...] = y_rows[...]

    def mine(n, at, lanes):
        return xo[0, n * 128 + at : n * 128 + at + 8, lanes]

    def others(n, at, lanes):
        return (xa, xb)[n][0, at : at + 8, lanes]

    place_rows(b, mask, t_ref, (0, 1), (mine, others))
    here = pl.ds(pl.multiple_of((b[3] * N_PAIR + b[4] * NH + b[5]) * 8, 8), 8)
    t_ref[here, 0:TILE] = t_ref[here, 0:TILE] + diag[...]
    o_ref[...] = t_ref[...].T


def assemble(name, kernel, mask, parts, out_shape, scratch, weight=1, after=()):
    def body(*refs):
        n_in = 1 + len(parts)
        kernel(*refs[:n_in], *refs[n_in + len(after) :])

    return pl.pallas_call(
        body,
        in_specs=[pl.BlockSpec(memory_space=pltpu.SMEM)] + [VMEM] * len(parts) + [ANY] * len(after),
        out_specs=VMEM,
        out_shape=jax.ShapeDtypeStruct(out_shape, F32),
        scratch_shapes=[pltpu.VMEM(shape, F32) for shape in scratch],
        cost_estimate=pl.CostEstimate(
            flops=1000000000 * weight, bytes_accessed=4 * QB * 1024, transcendentals=0
        ),
        compiler_params=pltpu.CompilerParams(vmem_limit_bytes=LIMIT),
        name=name,
    )(mask, *parts, *after)


def energy_tile(pair_list, valence_energy, conduction_energy):
    table = jnp.arange(valence_energy.shape[0], dtype=jnp.int32)
    cond_hits = pair_list[:, 1][:, None] == table[None, :]
    val_hits = pair_list[:, 0][:, None] == table[None, :]
    energy = jnp.sum(jnp.where(cond_hits, conduction_energy[None, :], 0.0), axis=1) - jnp.sum(
        jnp.where(val_hits, valence_energy[None, :], 0.0), axis=1
    )
    return jnp.eye(8, TILE, dtype=F32) * energy[:, None]


def per_device(densities, coulomb, pair_list, valence_energy, conduction_energy, tile_mask):
    swap = lambda a: lax.ppermute(a, "comp", CORE)
    zmove = lambda a: lax.ppermute(a, ("comp", "pair"), ZSPLIT)
    with jax.named_scope("panel"):
        v = pick(densities, coulomb)
        w = swap(v)
        held, w = lax.optimization_barrier((densities, w))
        dens = (densities, swap(held))
        vw, vw_again = pair_up(v, w)
        hvw = lax.ppermute(vw_again, "pair", HALF)
        near = zmove(vw)
        near2 = zmove(hvw)
    early = (vw, hvw)

    ahead = lambda a: lax.ppermute(a, "comp", AHEAD)
    behind = lambda a: lax.ppermute(a, "comp", BEHIND)
    across = lambda a: lax.ppermute(a, "comp", XSWAP)

    def both(out, start, other_x, dy, terms=()):
        return [
            (
                out, start + n if isinstance(start, int) else tuple(s if s is None else s + n for s in start),
                lambda b, n=n: block_of(b, other_x, dy) + n,
                tuple((a, lambda b, g=0, t=t, n=n: (t[g] if isinstance(t, tuple) else t) + n) for a, t in terms),
            )
            for n in range(NC)
        ]

    def each(out_mine, out_other, other_x, terms):
        mine, other = lambda b: b[2], lambda b: 1 - b[2]
        return [
            (
                out, 0,
                lambda b, core=core: block_of(b, other_x, 0) + core(b),
                tuple(
                    (a, lambda b, g=0, t=t, core=core: (t[g] if isinstance(t, tuple) else t) + core(b))
                    for a, t in terms
                ),
            )
            for out, core in ((out_mine, mine), (out_other, other))
        ]

    def mmx(name, *rest, **more):
        return mm(name, [(near2,), (far,)], dens, *rest, **more)

    def mmy(name, *rest, **more):
        return mm(name, [early, (near,)], dens, *rest, **more)

    def through_y(other_x, **more):
        dest = lambda out, start, dy: both(out, start, other_x, dy)
        m1, m2 = mmy("m12y", dest(0, 0, 2) + dest(1, 0, -1), [(2, BF16, 0)] * 2, **more)
        return m1, ahead(m1), behind(m2)

    def through_y_2(other_x, m1r, after):
        m3, = mmy("m3y", both(0, 0, other_x, 1, [(0, 0)]), [(2, BF16, 0)], [m1r], after=after)
        return m3, ahead(m3)

    near_dests = both(0, 0, True, 2) + both(0, 2, True, -1)
    with jax.named_scope("y_then_x"):
        m1o, m1or, m2or = through_y(True)
    with jax.named_scope("x_then_y_send"):
        chosen = choose(near, near2, m1o)
        far = zmove(chosen)
        xe, = mm(
            "xe", [(near2,)], dens, near_dests + both(0, 4, True, 1), [(6, BF16, 0)], after=(chosen,)
        )
        xer = across(xe)
    with jax.named_scope("y_then_x"):
        m1w, m1wr, m2wr = through_y(False, after=(xe,))
    with jax.named_scope("x_then_y_send"):
        xl, = mm("xl", [(far,)], dens, near_dests, [(4, BF16, 0)], after=(m1w, m1or, m2or), weight=100)
        xlr = across(xl)
    with jax.named_scope("y_then_x"):
        m3o, m3or = through_y_2(True, m1or, (xl, m2or))
        x3, = mmx(
            "x3", both(0, (None, 0), True, 1) + both(0, (2, 4), True, 0), [(6, BF16, 128)], after=(m3o,)
        )
        x3r = across(x3)
        m3w, m3wr = through_y_2(False, m1wr, (x3, m2wr))
    with jax.named_scope("x_then_y"):
        m1x, m2x = mmx(
            "m12x", both(0, 0, False, 2, [((0, 1), 0)]) + both(1, 0, False, -1, [((0, 1), 2)]),
            [(2, BF16, 0)] * 2, [xer, xlr], after=(m3w,),
        )
        m1xr, m2xr = ahead(m1x), behind(m2x)
        yf, yg = mmy(
            "yfg", each(0, 1, True, [(0, 0), (1, 0)]), [(1, BF16, 0)] * 2, [m3or, m2or], after=(m1x, m2wr)
        )
        fo, fr = across(yf), lax.ppermute(yg, "comp", XCROSS)
    split = [(1, F32, 0)] + [(1, F32, 128)] * 2
    with jax.named_scope("last"):
        yo, *ys = mmy(
            "yos", each(0, (1, 2), False, [(0, 0), (1, 0)]), split, [m3wr, m2wr], after=(yf,)
        )
        yr = [swap(a) for a in ys]
        m3x, = mmx(
            "m3x", both(0, 0, False, 1, [((0, 1), (4, 0)), (2, 0)]), [(2, BF16, 0)], [xer, x3r, m1xr], after=(yo, *yr)
        )
        m3xr = ahead(m3x)
        window = 8 * N_COMP * N_PAIR
        xo, *xs = mmx(
            "xos", each(0, (1, 2), False, [((0, 0), (2, 4)), (1, 0), (2, 0)]), split, [x3r, m3xr, m2xr],
            after=(yo, m3x),
        )
        xr = [swap(a) for a in xs]
        y_rows = assemble(
            "gather_y", gather_y_kernel, tile_mask, (yo, *yr, fo, fr), (window, QB), (), 1, (xo,)
        )
        diag = energy_tile(pair_list, valence_energy, conduction_energy)
        return assemble(
            "final", final_kernel, tile_mask, (y_rows, xo, *xr, diag), (QB, window), [(window, QB)]
        )


def solution(mesh):
    return jax.shard_map(
        per_device,
        mesh=mesh,
        in_specs=(
            P("comp", "pair"),
            P(),
            P(("comp", "pair"), None),
            P(),
            P(),
            P(("pair", "comp"), None),
        ),
        out_specs=P(("pair", "comp"), None),
        check_vma=False,
    )
```

```python
import functools

import jax
import jax.numpy as jnp
from jax import lax
from jax.experimental import pallas as pl
from jax.experimental.pallas import tpu as pltpu
from jax.sharding import PartitionSpec as P

TILE = 128
NX, NY, NC = 2, 4, 2
NZ, NH = 4, 2
N_COMP, N_PAIR = NX * NY * NC, NZ * NH
QB = 512
F32, BF16 = jnp.float32, jnp.bfloat16


def comp_at(x, y, k):
    return ((x % NX) * NY + y % NY) * NC + k % NC


def comp_perm(move):
    out = []
    for c in range(N_COMP):
        x, y, k = c // (NY * NC), (c // NC) % NY, c % NC
        out.append((c, comp_at(*move(x, y, k))))
    return out


CORE = comp_perm(lambda x, y, k: (x, y, k + 1))
XSWAP = comp_perm(lambda x, y, k: (x + 1, y, k))
XCROSS = comp_perm(lambda x, y, k: (x + 1, y, k + 1))
AHEAD = comp_perm(lambda x, y, k: (x, y + 1 - 2 * k, k))
BEHIND = comp_perm(lambda x, y, k: (x, y - 1 + 2 * k, k))
HALF = [(p, p ^ 1) for p in range(N_PAIR)]
ZSPLIT = [
    (c * N_PAIR + p, c * N_PAIR + ((p // NH + 1 - 2 * (c % NC)) % NZ) * NH + p % NH)
    for c in range(N_COMP)
    for p in range(N_PAIR)
]


def place_facts():
    comp, pair = lax.axis_index("comp"), lax.axis_index("pair")
    return [comp // (NY * NC), (comp // NC) % NY, comp % NC, comp, pair // NH, pair % NH]


def step_sign(b):
    return 1 - 2 * b[2]


def block_of(b, other_x, dy):
    x = 1 - b[0] if other_x else b[0]
    return (x * NY + ((b[1] + dy * step_sign(b) + NY) % NY)) * NC


VMEM = pl.BlockSpec(memory_space=pltpu.VMEM)
ANY = pl.BlockSpec(memory_space=pl.ANY)
HBM = pl.BlockSpec(memory_space=pltpu.HBM)
LIMIT = 20 << 20
NO_ROOM = 58 << 20


def pick_kernel(dens, w_ref, o_ref, buf, sems):
    def load(n):
        return pltpu.make_async_copy(
            dens.at[:, n * QB : n * QB + TILE], buf.at[:, n * TILE : (n + 1) * TILE], sems.at[n]
        )

    for n in range(N_COMP):
        load(n).start()
    k, wide = buf.shape
    at = lax.broadcasted_iota(jnp.int32, (wide, TILE), 0)
    to = lax.broadcasted_iota(jnp.int32, (wide, TILE), 1)
    spots = (at == (to // 8) * TILE + to % 8).astype(BF16)
    per = k // TILE
    comp = lax.axis_index("comp")
    w = [w_ref[pl.ds(comp * per + n, 1), :] for n in range(per)]
    for n in range(N_COMP):
        load(n).wait()
    rows = jnp.dot(buf[...], spots, preferred_element_type=F32)
    o_ref[0] = (rows.T * jnp.concatenate(w, axis=1)).astype(BF16)


def pick(dens, coulomb):
    k = dens.shape[0]
    return pl.pallas_call(
        pick_kernel,
        in_specs=[HBM, VMEM],
        out_specs=VMEM,
        out_shape=jax.ShapeDtypeStruct((1, 8 * N_COMP, k), BF16),
        scratch_shapes=[
            pltpu.VMEM((k, N_COMP * TILE), BF16),
            pltpu.SemaphoreType.DMA((N_COMP,)),
        ],
        compiler_params=pltpu.CompilerParams(vmem_limit_bytes=LIMIT),
        name="pick",
    )(dens, coulomb.reshape(coulomb.shape[0] // TILE, TILE))


def pair_kernel(a_ref, b_ref, o_ref, same_ref):
    for out in (o_ref, same_ref):
        out[0:1] = a_ref[...]
        out[1:2] = b_ref[...]


def pair_up(a, b):
    return pl.pallas_call(
        pair_kernel,
        in_specs=[VMEM, VMEM],
        out_specs=[VMEM, VMEM],
        out_shape=[jax.ShapeDtypeStruct((2, *a.shape[1:]), a.dtype)] * 2,
        compiler_params=pltpu.CompilerParams(vmem_limit_bytes=LIMIT),
        name="pair_up",
    )(a, b)


def choose_kernel(zero, one, after, o_ref):
    o_ref[...] = jnp.where(place_facts()[2] == 0, zero[...], one[...])


def choose(zero, one, after):
    return pl.pallas_call(
        choose_kernel,
        in_specs=[VMEM, VMEM, ANY],
        out_specs=VMEM,
        out_shape=jax.ShapeDtypeStruct(zero.shape, zero.dtype),
        compiler_params=pltpu.CompilerParams(vmem_limit_bytes=LIMIT),
        name="choose",
    )(zero, one, after)


def mm_kernel(work, sizes, n_add, n_out, *refs):
    n_panel = sum(sizes)
    panels, (own, oth), refs = refs[:n_panel], refs[n_panel : n_panel + 2], refs[n_panel + 2 :]
    adds, outs = refs[:n_add], refs[n_add : n_add + n_out]
    own_buf, oth_buf, sems = refs[-3:]
    b = place_facts()

    def loads(n):
        at = pl.ds(pl.multiple_of(work[n][2](b) * QB, QB), QB)
        return [
            pltpu.make_async_copy(src.at[:, at], buf.at[n], sems.at[s, n])
            for s, (src, buf) in enumerate(((own, own_buf), (oth, oth_buf)))
        ]

    for n in range(len(work)):
        for copy in loads(n):
            copy.start()
    sides = ([], [])
    for size in sizes:
        group, panels = panels[:size], panels[size:]
        for n, side in enumerate(sides):
            if size == 1:
                side.append(group[0][n])
            else:
                side.append(jnp.where(b[2] == 0, group[0][n], group[1][n]))
    left, right = [jnp.concatenate(side) if len(side) > 1 else side[0] for side in sides]
    rows = left.shape[0]
    part = rows // len(sizes)
    for n, (out, slot, _, terms) in enumerate(work):
        for copy in loads(n):
            copy.wait()
        acc = jnp.dot(left, own_buf[n], preferred_element_type=F32)
        acc += jnp.dot(right, oth_buf[n], preferred_element_type=F32)
        for g in range(len(sizes)):
            piece = acc[g * part : (g + 1) * part]
            for a, where in terms:
                if isinstance(a, tuple):
                    piece += adds[a[g]][where(b, g)].astype(F32)
                else:
                    piece += adds[a][where(b), g * part : (g + 1) * part].astype(F32)
            if isinstance(out, tuple):
                step = rows // len(out)
                for m in range(g * part // step, (g + 1) * part // step):
                    outs[out[m]][slot] = piece[m * step - g * part : (m + 1) * step - g * part]
            elif isinstance(slot, tuple):
                if slot[g] is not None:
                    outs[out][slot[g]] = piece.astype(outs[out].dtype)
            else:
                outs[out][slot, g * part : (g + 1) * part] = piece.astype(outs[out].dtype)


def mm(name, groups, dens, work, outs, adds=(), after=(), limit=LIMIT, weight=1):
    k = dens[0].shape[0]
    rows = 128 * len(groups)
    n = len(work)
    panels = [piece for group in groups for piece in group]

    def body(*refs):
        n_in = len(panels) + 2 + len(adds)
        mm_kernel(
            work, [len(g) for g in groups], len(adds), len(outs), *refs[:n_in], *refs[n_in + len(after) :]
        )

    return pl.pallas_call(
        body,
        in_specs=[VMEM] * len(panels) + [HBM] * 2 + [VMEM] * len(adds) + [ANY] * len(after),
        out_specs=[VMEM] * len(outs),
        out_shape=[jax.ShapeDtypeStruct((m, out_rows or rows, QB), dtype) for m, dtype, out_rows in outs],
        scratch_shapes=[pltpu.VMEM((n, k, QB), BF16)] * 2 + [pltpu.SemaphoreType.DMA((2, n))],
        cost_estimate=pl.CostEstimate(
            flops=4 * n * rows * k * QB * weight, bytes_accessed=4 * n * k * QB, transcendentals=0
        ),
        compiler_params=pltpu.CompilerParams(vmem_limit_bytes=limit),
        name=name,
    )(*panels, *dens, *adds, *after)


ORDER = (((-1, 1), (-2, 0), (0, 0), (-1, 0)), ((1, 1), (2, 1), (0, 1), (1, 0)))


def place_rows(b, mask, t_ref, groups, sources):
    for source, rows_at in enumerate(sources):
        for n, g in enumerate(groups):
            spots = [
                ((b[4] + ORDER[s][g][0] + NZ) % NZ) * NH + (b[5] + ORDER[s][g][1]) % NH
                for s in range(2)
            ]
            same = b[2] if source == 0 else 1 - b[2]
            p = jnp.where(same == 0, spots[0], spots[1])
            for c in range(N_COMP):
                at = pl.ds(pl.multiple_of((c * N_PAIR + p) * 8, 8), 8)
                for t in range(QB // TILE):
                    lanes = slice(t * TILE, (t + 1) * TILE)
                    scale = (2 * mask[t, c]).astype(F32)
                    t_ref[at, lanes] = rows_at(n, c * 8, lanes) * scale


def gather_y_kernel(mask, yo, ya, yb, fo, fr, t_ref):
    def mine(n, at, lanes):
        row = slice(n * 128 + at, n * 128 + at + 8)
        return yo[0, row, lanes] + fo[0, row, lanes].astype(F32)

    def others(n, at, lanes):
        row = slice(n * 128 + at, n * 128 + at + 8)
        return (ya, yb)[n][0, at : at + 8, lanes] + fr[0, row, lanes].astype(F32)

    place_rows(place_facts(), mask, t_ref, (2, 3), (mine, others))


def final_kernel(mask, y_rows, xo, xa, xb, diag, o_ref, t_ref):
    b = place_facts()
    t_ref[...] = y_rows[...]

    def mine(n, at, lanes):
        return xo[0, n * 128 + at : n * 128 + at + 8, lanes]

    def others(n, at, lanes):
        return (xa, xb)[n][0, at : at + 8, lanes]

    place_rows(b, mask, t_ref, (0, 1), (mine, others))
    here = pl.ds(pl.multiple_of((b[3] * N_PAIR + b[4] * NH + b[5]) * 8, 8), 8)
    t_ref[here, 0:TILE] = t_ref[here, 0:TILE] + diag[...]
    o_ref[...] = t_ref[...].T


def assemble(name, kernel, mask, parts, out_shape, scratch, weight=1, after=()):
    def body(*refs):
        n_in = 1 + len(parts)
        kernel(*refs[:n_in], *refs[n_in + len(after) :])

    return pl.pallas_call(
        body,
        in_specs=[pl.BlockSpec(memory_space=pltpu.SMEM)] + [VMEM] * len(parts) + [ANY] * len(after),
        out_specs=VMEM,
        out_shape=jax.ShapeDtypeStruct(out_shape, F32),
        scratch_shapes=[pltpu.VMEM(shape, F32) for shape in scratch],
        cost_estimate=pl.CostEstimate(
            flops=1000000000 * weight, bytes_accessed=4 * QB * 1024, transcendentals=0
        ),
        compiler_params=pltpu.CompilerParams(vmem_limit_bytes=LIMIT),
        name=name,
    )(mask, *parts, *after)


def energy_tile(pair_list, valence_energy, conduction_energy):
    table = jnp.arange(valence_energy.shape[0], dtype=jnp.int32)
    cond_hits = pair_list[:, 1][:, None] == table[None, :]
    val_hits = pair_list[:, 0][:, None] == table[None, :]
    energy = jnp.sum(jnp.where(cond_hits, conduction_energy[None, :], 0.0), axis=1) - jnp.sum(
        jnp.where(val_hits, valence_energy[None, :], 0.0), axis=1
    )
    return jnp.eye(8, TILE, dtype=F32) * energy[:, None]


def per_device(densities, coulomb, pair_list, valence_energy, conduction_energy, tile_mask):
    swap = lambda a: lax.ppermute(a, "comp", CORE)
    zmove = lambda a: lax.ppermute(a, ("comp", "pair"), ZSPLIT)
    with jax.named_scope("panel"):
        v = pick(densities, coulomb)
        w = swap(v)
        held, w = lax.optimization_barrier((densities, w))
        dens = (densities, swap(held))
        vw, vw_again = pair_up(v, w)
        hvw = lax.ppermute(vw_again, "pair", HALF)
        near = zmove(vw)
        near2 = zmove(hvw)
    early = (vw, hvw)

    ahead = lambda a: lax.ppermute(a, "comp", AHEAD)
    behind = lambda a: lax.ppermute(a, "comp", BEHIND)
    across = lambda a: lax.ppermute(a, "comp", XSWAP)

    def both(out, start, other_x, dy, terms=()):
        return [
            (
                out, start + n if isinstance(start, int) else tuple(s if s is None else s + n for s in start),
                lambda b, n=n: block_of(b, other_x, dy) + n,
                tuple((a, lambda b, g=0, t=t, n=n: (t[g] if isinstance(t, tuple) else t) + n) for a, t in terms),
            )
            for n in range(NC)
        ]

    def each(out_mine, out_other, other_x, terms):
        mine, other = lambda b: b[2], lambda b: 1 - b[2]
        return [
            (
                out, 0,
                lambda b, core=core: block_of(b, other_x, 0) + core(b),
                tuple(
                    (a, lambda b, g=0, t=t, core=core: (t[g] if isinstance(t, tuple) else t) + core(b))
                    for a, t in terms
                ),
            )
            for out, core in ((out_mine, mine), (out_other, other))
        ]

    def mmx(name, *rest, **more):
        return mm(name, [(near2,), (far,)], dens, *rest, **more)

    def mmy(name, *rest, **more):
        return mm(name, [early, (near,)], dens, *rest, **more)

    def through_y(other_x, **more):
        dest = lambda out, start, dy: both(out, start, other_x, dy)
        m1, m2 = mmy("m12y", dest(0, 0, 2) + dest(1, 0, -1), [(2, BF16, 0)] * 2, **more)
        return m1, ahead(m1), behind(m2)

    def through_y_2(other_x, m1r, after):
        m3, = mmy("m3y", both(0, 0, other_x, 1, [(0, 0)]), [(2, BF16, 0)], [m1r], after=after)
        return m3, ahead(m3)

    near_dests = both(0, 0, True, 2) + both(0, 2, True, -1)
    with jax.named_scope("y_then_x"):
        m1o, m1or, m2or = through_y(True)
    with jax.named_scope("x_then_y_send"):
        chosen = choose(near, near2, m1o)
        far = zmove(chosen)
        xe, = mm(
            "xe", [(near2,)], dens, near_dests + both(0, 4, True, 1), [(6, BF16, 0)], after=(chosen,)
        )
        xer = across(xe)
    with jax.named_scope("y_then_x"):
        m1w, m1wr, m2wr = through_y(False, after=(xe,))
    with jax.named_scope("x_then_y_send"):
        xl, = mm("xl", [(far,)], dens, near_dests, [(4, BF16, 0)], after=(m1w, m1or, m2or), weight=100)
        xlr = across(xl)
    with jax.named_scope("y_then_x"):
        m3o, m3or = through_y_2(True, m1or, (xl, m2or))
        x3, = mmx(
            "x3", both(0, (None, 0), True, 1) + both(0, (2, 4), True, 0), [(6, BF16, 128)], after=(m3o,)
        )
        x3r = across(x3)
        m3w, m3wr = through_y_2(False, m1wr, (x3, m2wr))
    with jax.named_scope("x_then_y"):
        m1x, m2x = mmx(
            "m12x", both(0, 0, False, 2, [((0, 1), 0)]) + both(1, 0, False, -1, [((0, 1), 2)]),
            [(2, BF16, 0)] * 2, [xer, xlr], after=(m3w,),
        )
        m1xr, m2xr = ahead(m1x), behind(m2x)
        yf, yg = mmy(
            "yfg", each(0, 1, True, [(0, 0), (1, 0)]), [(1, BF16, 0)] * 2, [m3or, m2or], after=(m1x, m2wr)
        )
        fo, fr = across(yf), lax.ppermute(yg, "comp", XCROSS)
    split = [(1, F32, 0)] + [(1, F32, 128)] * 2
    with jax.named_scope("last"):
        yo, *ys = mmy(
            "yos", each(0, (1, 2), False, [(0, 0), (1, 0)]), split, [m3wr, m2wr], after=(yf,)
        )
        yr = [swap(a) for a in ys]
        m3x, = mmx(
            "m3x", both(0, 0, False, 1, [((0, 1), (4, 0)), (2, 0)]), [(2, BF16, 0)], [xer, x3r, m1xr], after=(yo, *yr, m2xr), weight=100
        )
        m3xr = ahead(m3x)
        window = 8 * N_COMP * N_PAIR
        xo, *xs = mmx(
            "xos", each(0, (1, 2), False, [((0, 0), (2, 4)), (1, 0), (2, 0)]), split, [x3r, m3xr, m2xr],
            after=(yo, m3x),
        )
        xr = [swap(a) for a in xs]
        y_rows = assemble(
            "gather_y", gather_y_kernel, tile_mask, (yo, *yr, fo, fr), (window, QB), (), 1, (xo,)
        )
        diag = energy_tile(pair_list, valence_energy, conduction_energy)
        return assemble(
            "final", final_kernel, tile_mask, (y_rows, xo, *xr, diag), (QB, window), [(window, QB)]
        )


def solution(mesh):
    return jax.shard_map(
        per_device,
        mesh=mesh,
        in_specs=(
            P("comp", "pair"),
            P(),
            P(("comp", "pair"), None),
            P(),
            P(),
            P(("pair", "comp"), None),
        ),
        out_specs=P(("pair", "comp"), None),
        check_vma=False,
    )
```
